32 devices in a mesh: img: 16 (over z, x, core), fou: 2 (over y).
Axes of the slice: x: 2, y: 2, z: 4, core: 2. Of those that a mesh axis runs over, the one named last changes fastest.
Arguments:
- sky_estimate: float32 [4, 2048, 2048], P(None, 'img', 'fou'), may hold values from 0 to 2
- dual_coeffs: bfloat16 [4, 9, 2048, 2048], P(None, None, 'img', 'fou'), may hold values from -2 to 2
- dirty_image: float32 [4, 2048, 2048], P(None, 'img', 'fou'), may hold values from -4 to 4
- filters: float32 [8, 17], replicated, may hold values from -1.5 to 1.5
- thresholds: float32 [9], replicated, may hold values from 0.2 to 1.2
- facet_rows: int32 [16], P('img'), may hold values from 32 to 128, as said below
- tile_slots: int32 [4, 32, 6], P(None, 'img'), may hold values from 0 to 31, as said below
- tile_count: int32 [4, 32], P(None, 'img'), may hold values from 1 to 6, as said below
- gram_tiles: bfloat16 [4, 32, 6, 64, 64], P(None, 'img'), may hold values from -4 to 4
Outputs:
- image_next: float32 [4, 2048, 2048], P(None, 'img', 'fou')
- dual_next: bfloat16 [4, 9, 2048, 2048], P(None, None, 'img', 'fou')
The draws below stay inside these ranges and needn't reach their ends.
Inputs may be any that keep to these rules, and one draw needn't show every extreme that they name: `facet_rows`: facet f covers image rows f * 128 to (f + 1) * 128 - 1; some facet is full. `tile_slots`: the 6 entries of one channel and v-tile are distinct. `tile_count`: slots at or beyond the count hold no tile; in each channel some v-tile uses all 6 slots.
All inputs are finite; a program needn't handle non-finite values.
Results may differ from the reference program's by a relative error of at most 0.005.
Values may be sent and summed in bfloat16 or wider, within the bound.
A program may use at most 192 MiB of HBM per device.

```python
import math
import jax
import jax.numpy as jnp
from jax import lax

PIXELS = 2048
CHANNELS = 4
FRAMES = 9
RADIUS = 8
BLOCK = 64
SLOTS = 6
BLOCKS = 32
FACETS = 16
ROWS_IMG = 128


def draw_facet_rows(key, part):
    first, second = jax.random.split(jax.random.fold_in(key, 11))
    counts = jax.random.randint(first, (FACETS,), ROWS_IMG // 4, ROWS_IMG + 1)
    chosen = jax.random.randint(second, (), 0, FACETS)
    return jnp.where(jnp.arange(FACETS) == chosen, ROWS_IMG, counts).astype(jnp.int32)


def draw_tile_slots(key, part):
    scores = jax.random.randint(jax.random.fold_in(key, 23), (CHANNELS, BLOCKS, BLOCKS), 0, 1 << 20)
    scores = scores * BLOCKS + jnp.arange(BLOCKS, dtype=jnp.int32)[None, None, :]
    ordering = jnp.argsort(scores, axis=-1)
    return ordering[:, :, :SLOTS].astype(jnp.int32)


def draw_tile_count(key, part):
    first, second = jax.random.split(jax.random.fold_in(key, 37))
    counts = jax.random.randint(first, (CHANNELS, BLOCKS), 1, SLOTS + 1)
    chosen = jax.random.randint(second, (CHANNELS, 1), 0, BLOCKS)
    return jnp.where(jnp.arange(BLOCKS)[None, :] == chosen, SLOTS, counts).astype(jnp.int32)


def draw_gram_tiles(key, part):
    first, second = jax.random.split(jax.random.fold_in(key, 53))
    shape = (CHANNELS, BLOCKS, SLOTS, BLOCK, BLOCK)
    diagonal = jax.random.uniform(first, shape[:-1], jnp.float32, 0.5, 2.0)
    noise = jax.random.normal(second, shape, jnp.float32)
    noise = (noise + jnp.swapaxes(noise, -1, -2)) * (0.5 / BLOCK ** 0.5)
    identity = jnp.eye(BLOCK, dtype=jnp.float32)
    return (noise + identity * diagonal[..., None]).astype(jnp.bfloat16)


def level_of(key, shape, cuts, smallest, high):
    def one(axis_at, shards_of):
        heights = jax.random.uniform(jax.random.fold_in(jax.random.fold_in(key, 6), axis_at), (shards_of,), jnp.float32, smallest / len(cuts), high / len(cuts))
        return jnp.repeat(jnp.exp(heights), shape[axis_at] // shards_of).reshape((-1,) + (1,) * (len(shape) - axis_at - 1))

    loudness = one(*cuts[0])
    for cut in cuts[1:]:
        loudness = loudness * one(*cut)
    return loudness


def gaussian(stream_key, dims, spread, reach, pieces=(), kind=jnp.bfloat16):
    gain = level_of(stream_key, dims, pieces, -0.22, 0.18) if pieces else 1.0
    array = jax.random.normal(stream_key, dims, jnp.float32) * spread * gain
    return jnp.minimum(jnp.maximum(array, -reach), reach).astype(kind)


def setup_inputs(seed: int = 0) -> dict:
    keys = jax.random.split(jax.random.key(seed), 10)
    sky_estimate = jnp.clip(2.0 * jax.random.uniform(keys[0], (CHANNELS, PIXELS, PIXELS), jnp.float32) ** level_of(keys[0], (CHANNELS, PIXELS, PIXELS), ((1, 16), (2, 2)), -0.2, 0.2), 0.0, 2.0)
    dual_coeffs = gaussian(keys[1], (CHANNELS, FRAMES, PIXELS, PIXELS), 0.3, 2.0, ((2, 16), (3, 2)))
    dirty_image = gaussian(keys[2], (CHANNELS, PIXELS, PIXELS), 0.5, 4.0, ((1, 16), (2, 2)), jnp.float32)
    filters = gaussian(keys[3], (FRAMES - 1, 2 * RADIUS + 1), (2 * RADIUS + 1) ** -0.5, 1.5, (), jnp.float32)
    thresholds = jnp.clip(jnp.exp(jax.random.uniform(keys[4], (FRAMES,), jnp.float32, math.log(0.2), math.log(1.2))), 0.2, 1.2)
    facet_rows = draw_facet_rows(jax.random.fold_in(keys[9], 71), 0)
    tile_slots = draw_tile_slots(jax.random.fold_in(keys[9], 71), 0)
    tile_count = draw_tile_count(jax.random.fold_in(keys[9], 71), 0)
    gram_tiles = draw_gram_tiles(jax.random.fold_in(keys[9], 71), 0)
    return dict(sky_estimate=sky_estimate, dual_coeffs=dual_coeffs, dirty_image=dirty_image, filters=filters, thresholds=thresholds, facet_rows=facet_rows, tile_slots=tile_slots, tile_count=tile_count, gram_tiles=gram_tiles)


STEP_PRIMAL = 0.5
STEP_DUAL = 0.5
PRECISE = lax.Precision.HIGHEST

def correlate(planes, filter_taps):
    groups = filter_taps.shape[0]
    radius = (filter_taps.shape[1] - 1) // 2
    layout = ('NCHW', 'OIHW', 'NCHW')
    rowwise = lax.conv_general_dilated(planes, filter_taps[:, None, :, None], (1, 1), ((radius, radius), (0, 0)), dimension_numbers=layout, feature_group_count=groups, precision=PRECISE)
    return lax.conv_general_dilated(rowwise, filter_taps[:, None, None, :], (1, 1), ((0, 0), (radius, radius)), dimension_numbers=layout, feature_group_count=groups, precision=PRECISE)

def reference(sky_estimate, dual_coeffs, dirty_image, filters, thresholds, facet_rows, tile_slots, tile_count, gram_tiles):
    taps_len = 2 * RADIUS + 1
    identity_tap = (jnp.arange(taps_len, dtype=jnp.int32) == RADIUS).astype(jnp.float32)
    all_taps = jnp.concatenate([identity_tap[None, :], filters], axis=0)
    flipped = all_taps[:, ::-1]

    def synth_channel(frames_one):
        return lax.optimization_barrier(jnp.sum(correlate(frames_one[None], flipped)[0], axis=0))
    synthesis = lax.map(synth_channel, dual_coeffs.astype(jnp.float32))
    spectrum = jnp.fft.fft2(sky_estimate)
    by_tile = jnp.swapaxes(spectrum, 1, 2).reshape(CHANNELS, BLOCKS, BLOCK, BLOCKS, BLOCK)
    positions = jnp.broadcast_to(tile_slots[:, :, None, :, None], (CHANNELS, BLOCKS, BLOCK, SLOTS, BLOCK))
    picked = jnp.take_along_axis(by_tile, positions, axis=3)
    in_use = (jnp.arange(SLOTS, dtype=jnp.int32)[None, None, :] < tile_count[:, :, None]).astype(jnp.float32)
    masked = gram_tiles.astype(jnp.float32) * in_use[:, :, :, None, None]
    selector = (tile_slots[:, :, :, None] == jnp.arange(BLOCKS, dtype=jnp.int32)[None, None, None, :]).astype(jnp.float32) * in_use[:, :, :, None]

    def weigh_part(plane_part):
        product = jnp.einsum('cqvsa,cqsab->cqvsb', plane_part, masked, precision=PRECISE)
        placed = jnp.einsum('cqvsb,cqst->cqvtb', product, selector, precision=PRECISE)
        return jnp.swapaxes(placed.reshape(CHANNELS, PIXELS, PIXELS), 1, 2)
    weighted = lax.complex(weigh_part(jnp.real(picked).astype(jnp.float32)), weigh_part(jnp.imag(picked).astype(jnp.float32)))
    gram_image = jnp.real(jnp.fft.ifft2(weighted)).astype(jnp.float32)
    counter = jnp.arange(PIXELS, dtype=jnp.int32)
    live_rows = (counter % ROWS_IMG < facet_rows[counter // ROWS_IMG]).astype(jnp.float32)
    image_next = jnp.maximum(sky_estimate - STEP_PRIMAL * (gram_image - dirty_image + synthesis), 0.0) * live_rows[None, :, None]
    probe = 2.0 * image_next - sky_estimate

    def update_frame(item):
        frame_taps, bound, current = item
        coeffs = correlate(probe[:, None], frame_taps[None, :])[:, 0]
        candidate = current.astype(jnp.float32) + STEP_DUAL * coeffs
        magnitude = jnp.sqrt(lax.optimization_barrier(jnp.sum(candidate * candidate, axis=0)))
        return (candidate * (bound / jnp.maximum(magnitude, bound))).astype(jnp.bfloat16)
    dual_next = jnp.swapaxes(lax.map(update_frame, (all_taps, thresholds, jnp.swapaxes(dual_coeffs, 0, 1))), 0, 1)
    return (image_next, dual_next)
```

```python
import functools
import math

import jax
import jax.numpy as jnp
import numpy as np
from jax import lax
from jax.experimental import pallas as pl
from jax.experimental.pallas import tpu as pltpu
from jax.sharding import PartitionSpec as P

STEP_PRIMAL = 0.5
STEP_DUAL = 0.5
LANES = 128
BF16 = jnp.bfloat16
F32 = jnp.float32


def dot(a, b, dims=((1,), (0,)), **kw):
    return lax.dot_general(a, b, (dims, ((), ())), preferred_element_type=F32, **kw)


def flip_halves(x):
    half = x.shape[-1] // 2
    return jnp.concatenate([x[:, half:], x[:, :half]], axis=1)


def half_sign(rows, lanes, dtype=F32):
    lane = lax.broadcasted_iota(jnp.int32, (rows, lanes), 1)
    return jnp.where(lane < lanes // 2, 1.0, -1.0).astype(dtype)


def tables(line, block):
    small = np.arange(block)[:, None] * np.arange(line)[None, :] % line
    angle = small * (2.0 * math.pi / line)
    by_row = np.concatenate([np.cos(angle), np.sin(angle)], axis=0).astype(np.float32)
    period = line // block
    turn = np.arange(period)[:, None] * np.arange(period)[None, :] % period
    turn = turn * (2.0 * math.pi / period)
    return by_row, np.cos(turn).astype(np.float32), np.sin(turn).astype(np.float32)


def turned(base, other, cos_tile, sin_tile):
    rows, lanes = base.shape
    period = cos_tile.shape[0]
    base = base.reshape(rows // period, period, lanes)
    other = other.reshape(rows // period, period, lanes)
    out = base * cos_tile[None] + other * sin_tile[None]
    return out.reshape(rows, lanes).astype(BF16)


def forward_kernel(x_ref, et_ref, es_ref, pc_ref, ps_ref, o_ref):
    both = [turned(et_ref[...], es_ref[...], pc_ref[i], ps_ref[i]) for i in range(2)]
    lanes = et_ref.shape[1]
    out = dot(x_ref[...], jnp.concatenate(both, axis=1))
    sign = half_sign(1, lanes)
    for i in range(2):
        o_ref[i] = (out[:, i * lanes : (i + 1) * lanes] * sign).astype(BF16)


def forward(x, et, es, pc, ps):
    rows, line = x.shape
    tiles, period, lanes = pc.shape
    whole = pl.BlockSpec((line, lanes), lambda i: (0, 0))
    turn = pl.BlockSpec((2, period, lanes), lambda i: (i, 0, 0))
    return pl.pallas_call(
        forward_kernel,
        grid=(tiles // 2,),
        in_specs=[pl.BlockSpec((rows, line), lambda i: (0, 0)), whole, whole, turn, turn],
        out_specs=pl.BlockSpec((2, rows, lanes), lambda i: (i, 0, 0)),
        out_shape=jax.ShapeDtypeStruct((tiles, rows, lanes), BF16),
        name="forward",
    )(x, et, es, pc, ps)


def backward_kernel(scale, y_ref, et_ref, es_ref, pc_ref, ps_ref, o_ref, all_y, table):
    tiles, rows, lanes = y_ref.shape

    @pl.when(pl.program_id(0) == 0)
    def _():
        sign = half_sign(1, lanes)
        for q in range(tiles):
            all_y[:, q * lanes : (q + 1) * lanes] = (y_ref[q].astype(F32) * sign).astype(BF16)

    for q in range(tiles):
        table[:, q * lanes : (q + 1) * lanes] = turned(
            et_ref[...], es_ref[...], pc_ref[q], ps_ref[q]
        )
    out = dot(all_y[...], table[...], ((1,), (1,)))
    o_ref[...] = (out * scale).astype(BF16)


def backward(y, et, es, pc, ps, scale):
    tiles, rows, lanes = y.shape
    line = et.shape[0]
    part = min(256, line)
    chunk = pl.BlockSpec((part, lanes), lambda i: (i, 0))
    fixed = pl.BlockSpec(pc.shape, lambda i: (0, 0, 0))
    return pl.pallas_call(
        functools.partial(backward_kernel, scale),
        grid=(line // part,),
        in_specs=[pl.BlockSpec((tiles, rows, lanes), lambda i: (0, 0, 0)), chunk, chunk, fixed, fixed],
        out_specs=pl.BlockSpec((rows, part), lambda i: (0, i)),
        out_shape=jax.ShapeDtypeStruct((rows, line), BF16),
        scratch_shapes=[
            pltpu.VMEM((rows, tiles * lanes), BF16),
            pltpu.VMEM((part, tiles * lanes), BF16),
        ],
        name="backward",
    )(y, et, es, pc, ps)


def gram_kernel(slots_ref, x_ref, g_ref, e_ref, et_ref, es_ref, rc_ref, rs_ref, pc_ref, ps_ref,
                o_ref, table, table_t):
    c = pl.program_id(0)
    parts, _, rows, lanes = x_ref.shape
    wide, line = e_ref.shape
    block = wide // 2
    slots = g_ref.shape[1]
    x = x_ref[:, 0].reshape(parts * rows, lanes)
    top, low = e_ref[:block], e_ref[block:]
    for k in range(slots):
        t = slots_ref[c, k]
        cos_row = rc_ref[pl.ds(t, 1), :]
        sin_row = rs_ref[pl.ds(t, 1), :]
        table[k * wide : k * wide + block] = (top * cos_row - low * sin_row).astype(BF16)
        table[k * wide + block : (k + 1) * wide] = (low * cos_row + top * sin_row).astype(BF16)
        table_t[:, k * wide : (k + 1) * wide] = turned(
            et_ref[...], es_ref[...], pc_ref[t], ps_ref[t]
        )
    first = dot(table[...], x)
    sign = half_sign(1, lanes)
    stack = []
    for k in range(slots):
        cos_part = first[k * wide : k * wide + block]
        sin_part = first[k * wide + block : (k + 1) * wide]
        spec = cos_part + flip_halves(sin_part) * sign
        out = dot(g_ref[0, k], spec, precision=lax.Precision.HIGHEST)
        stack += [out, flip_halves(out) * -sign]
    stack = jnp.concatenate(stack, axis=0)
    high = stack.astype(BF16)
    low_part = (stack - high.astype(F32)).astype(BF16)
    back = dot(table_t[...], high) + dot(table_t[...], low_part)
    o_ref[:, 0] = back.astype(BF16).reshape(parts, rows, lanes)


def gram(x, slots, g_t, e, et, es, rc, rs, pc, ps):
    parts, channels, rows, lanes = x.shape
    wide, line = e.shape
    count = g_t.shape[1]

    def fixed(a):
        return pl.BlockSpec(a.shape, lambda i, s: (0,) * a.ndim)

    data = pl.BlockSpec((parts, 1, rows, lanes), lambda i, s: (0, i, 0, 0))
    return pl.pallas_call(
        gram_kernel,
        grid_spec=pltpu.PrefetchScalarGridSpec(
            num_scalar_prefetch=1,
            grid=(channels,),
            in_specs=[
                data,
                pl.BlockSpec((1,) + g_t.shape[1:], lambda i, s: (i, 0, 0, 0)),
                fixed(e), fixed(et), fixed(es), fixed(rc), fixed(rs), fixed(pc), fixed(ps),
            ],
            out_specs=data,
            scratch_shapes=[
                pltpu.VMEM((count * wide, line), BF16),
                pltpu.VMEM((line, count * wide), BF16),
            ],
        ),
        out_shape=jax.ShapeDtypeStruct(x.shape, BF16),
        name="gram",
    )(slots, x, g_t, e, et, es, rc, rs, pc, ps)


def synthesis_kernel(d_ref, col_ref, row_ref, o_ref, across):
    _, frames, rows, cols = d_ref.shape
    parts = cols // LANES
    for f in range(frames):
        zero = jnp.zeros((rows, LANES), BF16)
        windows = [jnp.concatenate([zero, d_ref[0, f, :, :LANES]], axis=1)]
        for j in range(1, parts):
            windows.append(d_ref[0, f, :, (j - 1) * LANES : (j + 1) * LANES])
        windows.append(jnp.concatenate([d_ref[0, f, :, cols - LANES :], zero], axis=1))
        out = dot(jnp.concatenate(windows, axis=0), col_ref[f]).astype(BF16)
        for j in range(parts + 1):
            across[f * rows : (f + 1) * rows, j * LANES : (j + 1) * LANES] = out[
                j * rows : (j + 1) * rows
            ]
    o_ref[0] = dot(row_ref[...], across[...])


def synthesize(dual, col_band, row_band):
    channels, frames, rows, cols = dual.shape
    wide = cols + LANES
    tall = row_band.shape[0]
    return pl.pallas_call(
        synthesis_kernel,
        grid=(channels,),
        in_specs=[
            pl.BlockSpec((1, frames, rows, cols), lambda c: (c, 0, 0, 0)),
            pl.BlockSpec(col_band.shape, lambda c: (0, 0, 0)),
            pl.BlockSpec(row_band.shape, lambda c: (0, 0)),
        ],
        out_specs=pl.BlockSpec((1, tall, wide), lambda c: (c, 0, 0)),
        out_shape=jax.ShapeDtypeStruct((channels, tall, wide), F32),
        scratch_shapes=[pltpu.VMEM((frames * rows, wide), BF16)],
        cost_estimate=pl.CostEstimate(
            flops=channels * frames * rows * wide * 800, bytes_accessed=dual.size * 2, transcendentals=0
        ),
        name="synthesis",
    )(dual, col_band, row_band)


def analysis_kernel(bound_ref, p_ref, d_ref, col_ref, row_ref, o_ref, cand):
    channels, _, rows, cols = d_ref.shape
    tall = p_ref.shape[1]
    parts = cols // LANES
    bound = bound_ref[pl.program_id(0)]
    total = None
    for c in range(channels):
        windows = [p_ref[c, :, j * LANES : (j + 2) * LANES] for j in range(parts)]
        out = dot(jnp.concatenate(windows, axis=0), col_ref[0]).astype(BF16)
        across = jnp.concatenate([out[j * tall : (j + 1) * tall] for j in range(parts)], axis=1)
        new = d_ref[c, 0].astype(F32) + STEP_DUAL * dot(row_ref[0], across)
        cand[c] = new
        total = new * new if total is None else total + new * new
    scale = bound / jnp.maximum(jnp.sqrt(total), bound)
    for c in range(channels):
        o_ref[c, 0] = (cand[c] * scale).astype(BF16)


def analyse(probe, dual, col_band, row_band, bounds):
    channels, frames, rows, cols = dual.shape
    block = pl.BlockSpec((channels, 1, rows, cols), lambda f: (0, f, 0, 0))
    return pl.pallas_call(
        analysis_kernel,
        grid=(frames,),
        in_specs=[
            pl.BlockSpec(memory_space=pltpu.SMEM),
            pl.BlockSpec(probe.shape, lambda f: (0, 0, 0)),
            block,
            pl.BlockSpec((1,) + col_band.shape[1:], lambda f: (f, 0, 0)),
            pl.BlockSpec((1,) + row_band.shape[1:], lambda f: (f, 0, 0)),
        ],
        out_specs=block,
        out_shape=jax.ShapeDtypeStruct(dual.shape, BF16),
        scratch_shapes=[pltpu.VMEM((channels, rows, cols), F32)],
        name="analysis",
    )(bounds, probe, dual, col_band, row_band)


def banded(taps, offset):
    count = taps.shape[1]
    out = jnp.zeros((taps.shape[0],) + offset.shape, F32)
    for tap in range(count):
        hit = jnp.asarray(offset) == tap
        out = jnp.where(hit[None], taps[:, tap][:, None, None], out)
    return out.astype(BF16)


def shift_up(x, axis):
    count = lax.axis_size(axis)
    return lax.ppermute(x, axis, [(i, i + 1) for i in range(count - 1)])


def shift_down(x, axis):
    count = lax.axis_size(axis)
    return lax.ppermute(x, axis, [(i + 1, i) for i in range(count - 1)])


MESH = pl.DeviceIdType.MESH
HIGH = lax.Precision.HIGHEST
NT = ((1,), (1,))
TN = ((0,), (0,))


def lane_ids(rows, lanes):
    return lax.broadcasted_iota(jnp.int32, (rows, lanes), 1)


def swap(x):
    return pltpu.roll(x, x.shape[1] // 2, 1)


def split(x):
    high = x.astype(BF16).astype(F32)
    return high, x - high


def fft(xs, sign, side):
    n = len(xs)
    if n == 1:
        return xs
    even, odd = fft(xs[::2], sign, side), fft(xs[1::2], sign, side)
    low, high = [], []
    for k in range(n // 2):
        angle = sign * 2.0 * math.pi * k / n
        c, s = math.cos(angle), math.sin(angle)
        t = odd[k]
        if 4 * k == n:
            t = swap(t) * (side * s)
        elif k:
            t = t * c + swap(t) * (side * s)
        low.append(even[k] + t)
        high.append(even[k] - t)
    return low + high


def core_tables(line, n, block, slots):
    rows = line // n
    lanes = 2 * block
    tiles = line // block
    taps = block // n

    def trig(product, period):
        angle = (product % period) * (2.0 * math.pi / period)
        return np.cos(angle), np.sin(angle)

    s = np.arange(line)
    c, sn = trig(s[:, None] * np.arange(block)[None, :], line)
    base = np.concatenate([c, -sn], axis=1)
    c, sn = trig(np.arange(n)[:, None] * np.arange(n)[None, :], n)
    turn_c = np.broadcast_to(c[:, :, None], (n, n, lanes))
    turn_s = np.broadcast_to(sn[:, :, None], (n, n, lanes))
    small_c = np.zeros((n, lanes))
    small_s = np.zeros((n, lanes))
    small_c[:, :n], small_s[:, :n] = c, sn
    pair_c, pair_s = small_c.copy(), small_s.copy()
    pair_c[:, n : 2 * n], pair_s[:, n : 2 * n] = c, sn
    c, sn = trig((np.arange(n) * 2 + 1)[:, None] * block * s[None, :], line)
    edge = np.concatenate([c, -sn], axis=0)
    r = np.arange(rows)
    u = np.arange(n)[:, None] + n * np.arange(taps)[None, :]
    c, sn = trig(u[:, :, None] * r[None, None, :], line)
    real = np.concatenate([c, sn], axis=2)
    imag = np.concatenate([-sn, c], axis=2)
    phase = np.concatenate([real, imag], axis=1)
    phase2 = np.concatenate([imag, -real], axis=1)
    c, sn = trig(np.arange(tiles)[:, None] * block * r[None, :], line)
    tile_c = np.zeros((lanes, 2 * rows))
    tile_s = np.zeros((lanes, 2 * rows))
    tile_c[:tiles] = np.concatenate([c, c], axis=1)
    tile_s[:tiles] = np.concatenate([sn, sn], axis=1)
    where_row = np.arange(2 * block)
    b = where_row // (2 * taps) + n * (where_row % taps)
    pick = (b[:, None] == np.arange(block)[None, :]).astype(np.float64)
    part = where_row // taps % 2
    same = (part[:, None] == part[None, :]).astype(np.float64)
    f32 = [base, turn_c, turn_s, small_c, small_s, pair_c, pair_s, phase, phase2, tile_c, tile_s, same]
    bf16 = [edge, pick, pick.T]
    return [np.ascontiguousarray(a, dtype=np.float32) for a in f32] + [
        np.ascontiguousarray(a, dtype=np.float32).astype(BF16) for a in bf16
    ]


def core_kernel(scale, sky, gram, slot, base, turn_c, turn_s, small_c, small_s, pair_c, pair_s,
                phase, phase2, tile_c, tile_s, same, edge, pick, pick_t, out,
                table, held, lines, sent, got, sent_e, got_e, gram_far, slot_far, left, right, tail,
                grow_c, grow_s, mid, wide, tail_sum, back, back_e, home, home_e, half, half_got,
                near_s, near_r, far_s, far_r, fwd_s, fwd_r, edge_s, edge_r, bwd_s, bwd_r,
                bedge_s, bedge_r, last_s, last_r):
    n, fou = lax.axis_size("img"), lax.axis_size("fou")
    devices = n * fou
    i, f = lax.axis_index("img"), lax.axis_index("fou")
    me = i * fou + f
    other = 1 - f
    partner = n - 1 - i
    chunks = lines.shape[0]
    rows, cols = sky.shape[1], sky.shape[2]
    slab = rows // fou
    lanes = base.shape[1]
    block = lanes // 2
    taps = block // n
    slots = gram.shape[2]
    line = cols * fou
    low = lane_ids(1, lanes) < block
    side = jnp.where(low, -1.0, 1.0).astype(F32)
    edge_lane = lane_ids(1, lanes) % block == 0
    all_lane = lane_ids(1, lanes)

    barrier = pltpu.get_barrier_semaphore()

    def greet(k, _):
        peer = (me + k) % devices
        pl.semaphore_signal(barrier, inc=1, device_id=(peer // fou, peer % fou), device_id_type=MESH)
        return 0

    lax.fori_loop(1, devices, greet, 0)

    def stage(p, _):
        mine = pl.ds(pl.multiple_of(f * slab, slab), slab)
        theirs = pl.ds(pl.multiple_of(other * slab, slab), slab)
        here = pl.ds(pl.multiple_of(f * cols, cols), cols)
        for q in range(fou):
            held[p, q * slab : (q + 1) * slab, :] = sky[p * fou + q, theirs, :].astype(BF16)
            lines[p, q * slab : (q + 1) * slab, here] = sky[p * fou + q, mine, :].astype(BF16)
        return 0

    lax.fori_loop(0, chunks, stage, 0)
    pl.semaphore_wait(barrier, devices - 1)

    def near_copy(p):
        here = pl.ds(pl.multiple_of(f * cols, cols), cols)
        return pltpu.make_async_remote_copy(
            src_ref=held.at[p], dst_ref=lines.at[p, :, here], send_sem=near_s.at[p],
            recv_sem=near_r.at[p], device_id=(i, other), device_id_type=MESH)

    def far_copies(p):
        return [
            pltpu.make_async_remote_copy(
                src_ref=gram.at[p * fou + f, 1], dst_ref=gram_far.at[p], send_sem=far_s.at[p, 0],
                recv_sem=far_r.at[p, 0], device_id=(partner, f), device_id_type=MESH),
            pltpu.make_async_remote_copy(
                src_ref=slot.at[p * fou + f, 1], dst_ref=slot_far.at[p], send_sem=far_s.at[p, 1],
                recv_sem=far_r.at[p, 1], device_id=(partner, f), device_id_type=MESH),
        ]

    def open_sends(p, _):
        near_copy(p).start()
        return 0

    def open_far(p, _):
        for copy in far_copies(p):
            copy.start()
        return 0

    lax.fori_loop(0, chunks, open_sends, 0)
    lax.fori_loop(0, chunks, open_far, 0)

    period = turn_c.shape[1]
    shape = (rows // period, period, lanes)

    def other_base(a, _):
        at = pl.ds(pl.multiple_of(a * rows, rows), rows)
        wide[a] = swap(base[at, :]) * -side
        return 0

    lax.fori_loop(0, n, other_base, 0)

    def fill(t, _):
        to = pl.ds(pl.multiple_of(t * lanes, lanes), lanes)
        c, s = turn_c[t][None], turn_s[t][None]

        def piece(a, _):
            at = pl.ds(pl.multiple_of(a * rows, rows), rows)
            value = base[at, :].reshape(shape) * c + wide[a].reshape(shape) * s
            table[at, to] = value.reshape(rows, lanes).astype(BF16)
            return 0

        lax.fori_loop(0, n, piece, 0)
        return 0

    lax.fori_loop(0, n, fill, 0)

    def fwd_copy(p, t, q):
        return pltpu.make_async_remote_copy(
            src_ref=sent.at[p, pl.ds(pl.multiple_of(q * slab, slab), slab), pl.ds(pl.multiple_of(t * lanes, lanes), lanes)],
            dst_ref=got.at[p, i, pl.ds(pl.multiple_of(f * slab, slab), slab), :],
            send_sem=fwd_s.at[p, t * fou + q], recv_sem=fwd_r.at[p, me],
            device_id=(t, q), device_id_type=MESH)

    def edge_copy(p, t, q):
        return pltpu.make_async_remote_copy(
            src_ref=sent_e.at[p, q, t], dst_ref=got_e.at[p, f, i],
            send_sem=edge_s.at[p, t * fou + q], recv_sem=edge_r.at[p, me],
            device_id=(t, q), device_id_type=MESH)

    def bwd_copy(p, t, q):
        return pltpu.make_async_remote_copy(
            src_ref=back.at[p, t, pl.ds(pl.multiple_of(q * slab, slab), slab), :],
            dst_ref=home.at[p, pl.ds(pl.multiple_of(f * slab, slab), slab),
                            pl.ds(pl.multiple_of(i * lanes, lanes), lanes)],
            send_sem=bwd_s.at[p, t * fou + q], recv_sem=bwd_r.at[p, me],
            device_id=(t, q), device_id_type=MESH)

    def bedge_copy(p, t, q):
        return pltpu.make_async_remote_copy(
            src_ref=back_e.at[p, q, t], dst_ref=home_e.at[p, f, i],
            send_sem=bedge_s.at[p, t * fou + q], recv_sem=bedge_r.at[p, me],
            device_id=(t, q), device_id_type=MESH)

    pairs = n // 2

    def forward_chunk(p, _):
        near_copy(p).wait_recv()
        x = lines[p]

        def tile(m, _):
            g = (i // 2 + pairs // 2 + m) % pairs
            at = pl.ds(pl.multiple_of(g * 2 * lanes, 2 * lanes), 2 * lanes)
            sent[p, :, at] = dot(lines[p], table[:, at]).astype(BF16)
            for a in range(2):
                for q in range(fou):
                    t = g * 2 + a
                    itself = (t == i) & (q == f)

                    @pl.when(jnp.logical_not(itself))
                    def _():
                        fwd_copy(p, t, q).start()

                    @pl.when(itself)
                    def _():
                        got[p, i, pl.ds(pl.multiple_of(f * slab, slab), slab), :] = sent[
                            p, q * slab : (q + 1) * slab, pl.ds(pl.multiple_of(t * lanes, lanes), lanes)]
            return 0

        lax.fori_loop(0, pairs, tile, 0)
        e = dot(edge[...], x, NT)
        er, ei = e[:n], e[n:]
        for q in range(fou):
            both = jnp.where(low, er, swap(ei)) if q == 0 else jnp.where(low, swap(er), ei)
            for t in range(n):
                sent_e[p, q, t] = both[t : t + 1]

        def send_edges(k, _):
            peer = (me + k) % devices
            edge_copy(p, peer // fou, peer % fou).start()
            return 0

        lax.fori_loop(1, devices, send_edges, 0)
        got_e[p, f, i] = sent_e[p, f, i]
        return 0

    lax.fori_loop(0, chunks, forward_chunk, 0)

    step = 16

    def gram_chunk(p, _):
        def arrive(k, _):
            peer = (me + k) % devices
            pltpu.make_async_remote_copy(
                src_ref=sent.at[p, 0:slab, 0:lanes],
                dst_ref=got.at[p, peer // fou, pl.ds(pl.multiple_of(peer % fou * slab, slab), slab), :],
                send_sem=fwd_s.at[p, peer], recv_sem=fwd_r.at[p, peer],
                device_id=(peer // fou, peer % fou), device_id_type=MESH).wait_recv()
            pltpu.make_async_remote_copy(
                src_ref=sent_e.at[p, 0, 0], dst_ref=got_e.at[p, peer % fou, peer // fou],
                send_sem=edge_s.at[p, peer], recv_sem=edge_r.at[p, peer],
                device_id=(peer // fou, peer % fou), device_id_type=MESH).wait_recv()
            return 0

        lax.fori_loop(1, devices, arrive, 0)

        def column(m, _):
            at = pl.ds(pl.multiple_of(m * step, step), step)
            below = pl.ds(pl.multiple_of(rows + m * step, step), step)
            xs = [got[p, t, at, :].astype(F32) for t in range(n)]
            for t, a in enumerate(fft(xs, -1.0, side)):
                high, rest = split(a)
                right[t, at, :] = jnp.where(low, high, swap(rest)).astype(BF16)
                right[t, below, :] = jnp.where(low, swap(high), rest).astype(BF16)
            return 0

        lax.fori_loop(0, rows // step, column, 0)
        e0 = jnp.concatenate([got_e[p, 0, t] for t in range(n)], axis=0)
        e1 = jnp.concatenate([got_e[p, 1, t] for t in range(n)], axis=0)
        zr = jnp.where(low, e0, swap(e1))
        zi = jnp.where(low, swap(e0), e1)
        for part in range(2):
            if part == 0:
                a = dot(zr, pair_c[...], TN, precision=HIGH) + dot(zi, pair_s[...], TN, precision=HIGH)
            else:
                a = dot(zi, pair_c[...], TN, precision=HIGH) - dot(zr, pair_s[...], TN, precision=HIGH)
            high, rest = split(a)
            tail[part * rows : (part + 1) * rows] = jnp.where(all_lane < n, high, rest).astype(BF16)

        for copy in far_copies(p):
            copy.wait_recv()
        for far in range(2):
            t = slot_far[p] if far else slot[p * fou + f, 0]
            hot = jnp.where(t == lane_ids(*t.shape).astype(F32), 1.0, 0.0)
            gc = dot(hot, tile_c[...], precision=HIGH)
            gs = dot(hot, tile_s[...], precision=HIGH)
            for k in range(slots):
                grow_c[far, k] = jnp.broadcast_to(gc[k : k + 1], (2 * taps, 2 * rows))
                grow_s[far, k] = jnp.broadcast_to(gs[k : k + 1], (2 * taps, 2 * rows))

        mirror = jnp.where(lane_ids(1, 2 * rows) < rows, 1.0, -1.0).astype(F32)
        deep = slots * 2 * taps

        def project(b, _):
            nb = (n - b) % n
            near = phase[b][None] * grow_c[0] + phase2[b][None] * grow_s[0]
            far = ((phase[nb] * mirror)[None] * grow_c[1] + (phase2[nb] * mirror)[None] * grow_s[1])
            left[b, :deep] = near.reshape(deep, 2 * rows).astype(BF16)
            left[b, deep:] = far.reshape(deep, 2 * rows).astype(BF16)
            both = dot(left[b], jnp.concatenate([right[b], tail[...]], axis=1))
            main = both[:, :lanes]
            main = main + swap(main)
            hit = (all_lane == b) | (all_lane == n + b)
            column = jnp.sum(jnp.where(hit, both[deep:, lanes:], 0.0), axis=1, keepdims=True)
            mirrored = jnp.where(edge_lane, column, main[deep:])
            width = 2 * taps
            mid[:slots, pl.ds(pl.multiple_of(b * width, width), width), :] = main[:deep].reshape(slots, width, lanes)
            mid[slots:, pl.ds(pl.multiple_of(nb * width, width), width), :] = mirrored.reshape(slots, width, lanes)
            return 0

        lax.fori_loop(0, n, project, 0)

        def weigh(k, far):
            g = gram_far[p, k] if far else gram[p * fou + f, 0, k]
            g = dot(pick[...], g, NT).astype(BF16)
            g = (dot(g, pick_t[...]) * same[...]).astype(BF16)
            at = slots + k if far else k
            high, rest = split(mid[at])
            w = dot(g, jnp.where(low, high, rest).astype(BF16))
            mid[at] = w + swap(w)

        for far in range(2):
            lax.fori_loop(0, slots, lambda k, _, far=far: (weigh(k, far), 0)[1], 0)

        tail_sum[...] = jnp.zeros_like(tail_sum)

        def spread(b, _):
            nb = (n - b) % n
            width = 2 * taps
            near = mid[:slots, pl.ds(pl.multiple_of(b * width, width), width), :].reshape(deep, lanes)
            far = mid[slots:, pl.ds(pl.multiple_of(nb * width, width), width), :].reshape(deep, lanes)
            column = far[:, 0:1]
            ch, cr = split(column)
            extra = jnp.where(all_lane == b, ch, jnp.where(all_lane == n + b, cr, 0.0))
            both = jnp.concatenate([near, jnp.where(edge_lane, 0.0, far)], axis=0)
            high, rest = split(both)
            extra = jnp.concatenate([jnp.zeros((deep, lanes), F32), extra], axis=0)
            rhs = jnp.concatenate([jnp.where(low, high, rest), extra], axis=1).astype(BF16)
            y = dot(left[b], rhs, TN)
            main = y[:, :lanes]
            main = main + swap(main)
            wide[b] = jnp.where(low, main[:rows], main[rows:])
            tail_sum[...] += y[:, lanes:]
            return 0

        lax.fori_loop(0, n, spread, 0)

        def uncolumn(m, _):
            at = pl.ds(pl.multiple_of(m * step, step), step)
            for t, a in enumerate(fft([wide[b, at, :] for b in range(n)], 1.0, side)):
                back[p, t, at, :] = a.astype(BF16)
            return 0

        lax.fori_loop(0, rows // step, uncolumn, 0)
        total = tail_sum[...]
        total = total + pltpu.roll(total, lanes - n, 1)
        br, bi = total[:rows], total[rows:]
        yr = dot(small_c[...], br, NT, precision=HIGH) - dot(small_s[...], bi, NT, precision=HIGH)
        yi = dot(small_s[...], br, NT, precision=HIGH) + dot(small_c[...], bi, NT, precision=HIGH)
        for q in range(fou):
            both = jnp.where(low, yr, swap(yi)) if q == 0 else jnp.where(low, swap(yr), yi)
            for t in range(n):
                back_e[p, q, t] = both[t : t + 1]

        def send_back(k, _):
            peer = (me + devices // 2 + k) % devices
            t, q = peer // fou, peer % fou

            @pl.when(peer != me)
            def _():
                bwd_copy(p, t, q).start()
                bedge_copy(p, t, q).start()

            return 0

        lax.fori_loop(0, devices, send_back, 0)
        home[p, pl.ds(pl.multiple_of(f * slab, slab), slab), pl.ds(pl.multiple_of(i * lanes, lanes), lanes)] = back[
            p, i, pl.ds(pl.multiple_of(f * slab, slab), slab), :]
        home_e[p, f, i] = back_e[p, f, i]
        return 0

    lax.fori_loop(0, chunks, gram_chunk, 0)

    def half_copy(p):
        return pltpu.make_async_remote_copy(
            src_ref=half.at[p], dst_ref=half_got.at[p], send_sem=last_s.at[p],
            recv_sem=last_r.at[p], device_id=(i, other), device_id_type=MESH)

    def backward_chunk(p, _):
        def arrive(k, _):
            peer = (me + k) % devices
            pltpu.make_async_remote_copy(
                src_ref=back.at[p, 0, 0:slab, :],
                dst_ref=home.at[p, pl.ds(pl.multiple_of(peer % fou * slab, slab), slab),
                                pl.ds(pl.multiple_of(peer // fou * lanes, lanes), lanes)],
                send_sem=bwd_s.at[p, peer], recv_sem=bwd_r.at[p, peer],
                device_id=(peer // fou, peer % fou), device_id_type=MESH).wait_recv()
            pltpu.make_async_remote_copy(
                src_ref=back_e.at[p, 0, 0], dst_ref=home_e.at[p, peer % fou, peer // fou],
                send_sem=bedge_s.at[p, peer], recv_sem=bedge_r.at[p, peer],
                device_id=(peer // fou, peer % fou), device_id_type=MESH).wait_recv()
            return 0

        lax.fori_loop(1, devices, arrive, 0)
        e0 = jnp.concatenate([home_e[p, 0, t] for t in range(n)], axis=0)
        e1 = jnp.concatenate([home_e[p, 1, t] for t in range(n)], axis=0)
        ext = jnp.concatenate(
            [jnp.where(low, e0, swap(e1)), jnp.where(low, swap(e0), e1)], axis=0).astype(BF16)
        part = 256

        def image(start):
            at = pl.ds(pl.multiple_of(start, part), part)
            y = dot(home[p], table[at, :], NT) + dot(ext, edge[:, at], TN)
            return y * scale

        def send_half(m, _):
            to = pl.ds(pl.multiple_of(m * part, part), part)
            half[p, :, to] = image(other * cols + m * part).astype(BF16)
            return 0

        lax.fori_loop(0, cols // part, send_half, 0)
        half_copy(p).start()

        def keep_half(m, _):
            to = pl.ds(pl.multiple_of(m * part, part), part)
            y = image(f * cols + m * part)
            for q in range(fou):
                out[p * fou + q, pl.ds(pl.multiple_of(f * slab, slab), slab), to] = y[q * slab : (q + 1) * slab]
            return 0

        lax.fori_loop(0, cols // part, keep_half, 0)
        return 0

    lax.fori_loop(0, chunks, backward_chunk, 0)

    def close(p, _):
        half_copy(p).wait_recv()
        for q in range(fou):
            out[p * fou + q, pl.ds(pl.multiple_of(other * slab, slab), slab), :] = half_got[
                p, q * slab : (q + 1) * slab, :].astype(F32)
        half_copy(p).wait_send()
        near_copy(p).wait_send()
        for copy in far_copies(p):
            copy.wait_send()

        def sent_all(k, _):
            peer = (me + k) % devices
            pltpu.make_async_remote_copy(
                src_ref=sent.at[p, 0:slab, 0:lanes], dst_ref=got.at[p, 0, 0:slab, :],
                send_sem=fwd_s.at[p, peer], recv_sem=fwd_r.at[p, peer],
                device_id=(peer // fou, peer % fou), device_id_type=MESH).wait_send()
            pltpu.make_async_remote_copy(
                src_ref=sent_e.at[p, 0, 0], dst_ref=got_e.at[p, 0, 0],
                send_sem=edge_s.at[p, peer], recv_sem=edge_r.at[p, peer],
                device_id=(peer // fou, peer % fou), device_id_type=MESH).wait_send()
            pltpu.make_async_remote_copy(
                src_ref=back.at[p, 0, 0:slab, :], dst_ref=home.at[p, 0:slab, 0:lanes],
                send_sem=bwd_s.at[p, peer], recv_sem=bwd_r.at[p, peer],
                device_id=(peer // fou, peer % fou), device_id_type=MESH).wait_send()
            pltpu.make_async_remote_copy(
                src_ref=back_e.at[p, 0, 0], dst_ref=home_e.at[p, 0, 0],
                send_sem=bedge_s.at[p, peer], recv_sem=bedge_r.at[p, peer],
                device_id=(peer // fou, peer % fou), device_id_type=MESH).wait_send()
            return 0

        lax.fori_loop(1, devices, sent_all, 0)
        return 0

    lax.fori_loop(0, chunks, close, 0)


def core(sky, gram, slot, line, n, fou, block):
    channels, rows, cols = sky.shape
    chunks = channels // fou
    slab = rows // fou
    lanes = 2 * block
    devices = n * fou
    slots = gram.shape[2]
    taps = block // n
    consts = core_tables(line, n, block, slots)
    vm = pl.BlockSpec(memory_space=pltpu.VMEM)
    dma = pltpu.SemaphoreType.DMA
    return pl.pallas_call(
        functools.partial(core_kernel, 1.0 / float(line * line)),
        in_specs=[vm] * (3 + len(consts)),
        out_specs=vm,
        out_shape=jax.ShapeDtypeStruct(sky.shape, F32),
        scratch_shapes=[
            pltpu.VMEM((line, line), BF16),
            pltpu.VMEM((chunks, fou * slab, cols), BF16),
            pltpu.VMEM((chunks, fou * slab, line), BF16),
            pltpu.VMEM((chunks, fou * slab, line), BF16),
            pltpu.VMEM((chunks, n, rows, lanes), BF16),
            pltpu.VMEM((chunks, fou, n, 1, lanes), F32),
            pltpu.VMEM((chunks, fou, n, 1, lanes), F32),
            pltpu.VMEM((chunks,) + gram.shape[2:], BF16),
            pltpu.VMEM((chunks,) + slot.shape[2:], F32),
            pltpu.VMEM((n, slots * 4 * taps, 2 * rows), BF16),
            pltpu.VMEM((n, 2 * rows, lanes), BF16),
            pltpu.VMEM((2 * rows, lanes), BF16),
            pltpu.VMEM((2, slots, 2 * taps, 2 * rows), F32),
            pltpu.VMEM((2, slots, 2 * taps, 2 * rows), F32),
            pltpu.VMEM((2 * slots, 2 * block, lanes), F32),
            pltpu.VMEM((n, rows, lanes), F32),
            pltpu.VMEM((2 * rows, lanes), F32),
            pltpu.VMEM((chunks, n, rows, lanes), BF16),
            pltpu.VMEM((chunks, fou, n, 1, lanes), F32),
            pltpu.VMEM((chunks, fou * slab, line), BF16),
            pltpu.VMEM((chunks, fou, n, 1, lanes), F32),
            pltpu.VMEM((chunks, fou * slab, cols), BF16),
            pltpu.VMEM((chunks, fou * slab, cols), BF16),
            dma((chunks,)), dma((chunks,)), dma((chunks, 2)), dma((chunks, 2)),
            dma((chunks, devices)), dma((chunks, devices)), dma((chunks, devices)), dma((chunks, devices)),
            dma((chunks, devices)), dma((chunks, devices)), dma((chunks, devices)), dma((chunks, devices)),
            dma((chunks,)), dma((chunks,)),
        ],
        compiler_params=pltpu.CompilerParams(collective_id=0, has_side_effects=True),
        name="core",
    )(sky, gram, slot, *consts)


def plain_gram(sky, tile_slots, tile_count, gram_tiles):
    channels, rows, cols = sky.shape
    fou = lax.axis_size("fou")
    img = lax.axis_size("img")
    devices = img * fou
    line = cols * fou
    block = gram_tiles.shape[-1]
    slots = gram_tiles.shape[2]
    tiles = line // block
    slab = rows // fou
    width = line // devices
    axes = ("img", "fou")

    by_row, cos_turn, sin_turn = tables(line, block)
    e = jnp.asarray(by_row)
    et = jnp.asarray(np.ascontiguousarray(by_row.T))
    es = jnp.concatenate([-et[:, block:], et[:, :block]], axis=1)
    lanes = 2 * block
    pc = jnp.broadcast_to(jnp.asarray(cos_turn)[:, :, None], (tiles, tiles, lanes))
    ps = jnp.broadcast_to(jnp.asarray(sin_turn)[:, :, None], (tiles, tiles, lanes))
    rc = jnp.tile(jnp.asarray(cos_turn), (1, line // tiles))
    rs = jnp.tile(jnp.asarray(sin_turn), (1, line // tiles))

    lines = lax.all_to_all(sky.astype(BF16), "fou", split_axis=1, concat_axis=2, tiled=True)
    spread = forward(lines.reshape(channels * slab, line), et, es, pc, ps)
    spread = spread.reshape(tiles, channels, slab, lanes)
    per = block // width
    if per > 1:
        spread = spread.reshape(tiles, channels, slab, 2, per, width)
        spread = spread.transpose(0, 4, 1, 2, 3, 5).reshape(devices, channels, slab, 2 * width)
    moved = lax.all_to_all(spread, axes, split_axis=0, concat_axis=0, tiled=True)

    which = lax.axis_index("fou") * width // block
    tile_g = lax.dynamic_index_in_dim(gram_tiles, which, 1, keepdims=False).astype(F32)
    chosen = lax.dynamic_index_in_dim(tile_slots, which, 1, keepdims=False)
    used = lax.dynamic_index_in_dim(tile_count, which, 1, keepdims=False)
    in_use = jnp.arange(slots)[None, :] < used[:, None]
    tile_g = jnp.where(in_use[:, :, None, None], jnp.swapaxes(tile_g, -1, -2), 0.0)

    if slab % 16:
        x = moved.transpose(1, 0, 2, 3).reshape(1, channels, line, 2 * width)
    else:
        x = moved
    y = gram(x, chosen, tile_g, e, et, es, rc, rs, pc, ps)
    if slab % 16:
        y = y.reshape(channels, devices, slab, 2 * width).transpose(1, 0, 2, 3)
    back = lax.all_to_all(y, axes, split_axis=0, concat_axis=0, tiled=True)
    if per > 1:
        back = back.reshape(tiles, per, channels, slab, 2, width).transpose(0, 2, 3, 4, 1, 5)
    back = back.reshape(tiles, channels * slab, lanes)
    final = backward(back, et, es, pc, ps, 1.0 / float(line * line))
    return lax.all_to_all(
        final.reshape(channels, slab, line), "fou", split_axis=2, concat_axis=1, tiled=True
    ).astype(F32)


def paired_gram(sky, tile_slots, tile_count, gram_tiles):
    line = sky.shape[2] * lax.axis_size("fou")
    slots = tile_slots.shape[2]
    used = jnp.arange(slots)[None, None, :] < tile_count[:, :, None]
    slot = jnp.where(used, tile_slots, -1).astype(F32)
    slot = jnp.pad(slot, ((0, 0), (0, 0), (0, -slots % 8)), constant_values=-1.0)
    slot = jnp.broadcast_to(slot[..., None], slot.shape + (2 * gram_tiles.shape[-1],))
    return core(sky, gram_tiles, slot, line, lax.axis_size("img"), lax.axis_size("fou"), gram_tiles.shape[-1])


def pairs_up(sky, gram_tiles):
    img, fou = lax.axis_size("img"), lax.axis_size("fou")
    channels, rows, cols = sky.shape
    line, block = cols * fou, gram_tiles.shape[-1]
    return (fou == 2 and channels % 2 == 0 and 2 * block == LANES and line == 2 * block * img
            and block % img == 0 and block // img == 4 and rows == LANES)


def body(sky, dual, dirty, filters, thresholds, facet_rows, tile_slots, tile_count, gram_tiles):
    channels, rows, cols = sky.shape
    taps_len = filters.shape[1]
    radius = (taps_len - 1) // 2
    fou = lax.axis_size("fou")
    img = lax.axis_size("img")
    devices = img * fou
    line = cols * fou
    block = gram_tiles.shape[-1]
    slots = gram_tiles.shape[2]
    tiles = line // block
    slab = rows // fou
    width = line // devices
    axes = ("img", "fou")

    identity = (jnp.arange(taps_len) == radius).astype(F32)
    taps = jnp.concatenate([identity[None], filters], axis=0)
    frames = taps.shape[0]
    tall = rows + 2 * radius
    near = np.arange(2 * LANES)[:, None]
    synth_col = banded(taps, np.arange(LANES)[None, :] + LANES - near)
    synth_row = banded(taps, np.arange(tall)[:, None] - np.arange(rows)[None, :])
    synth_row = synth_row.transpose(1, 0, 2).reshape(tall, frames * rows)
    ana_col = banded(taps, near - np.arange(LANES)[None, :])
    ana_row = banded(taps, np.arange(tall)[None, :] - np.arange(rows)[:, None])
    ext = synthesize(dual, synth_col, synth_row)
    mid = ext[:, :, radius : radius + cols]
    from_left = shift_up(ext[:, :, radius + cols : cols + 2 * radius], "fou")
    from_right = shift_down(ext[:, :, :radius], "fou")
    rest = cols - radius
    mid = mid + jnp.pad(from_left, ((0, 0), (0, 0), (0, rest))) + jnp.pad(
        from_right, ((0, 0), (0, 0), (rest, 0))
    )
    from_above = shift_up(mid[:, radius + rows :], "img")
    from_below = shift_down(mid[:, :radius], "img")
    rest = rows - radius
    synthesis = (
        mid[:, radius : radius + rows]
        + jnp.pad(from_above, ((0, 0), (0, rest), (0, 0)))
        + jnp.pad(from_below, ((0, 0), (rest, 0), (0, 0)))
    )

    find = paired_gram if pairs_up(sky, gram_tiles) else plain_gram
    gram_image = find(sky, tile_slots, tile_count, gram_tiles)

    live_rows = (jnp.arange(rows, dtype=jnp.int32) < facet_rows[0]).astype(F32)
    image_next = (
        jnp.maximum(sky - STEP_PRIMAL * (gram_image - dirty + synthesis), 0.0)
        * live_rows[None, :, None]
    )
    probe = (2.0 * image_next - sky).astype(BF16)
    probe = jnp.concatenate(
        [shift_up(probe[:, rows - radius :], "img"), probe, shift_down(probe[:, :radius], "img")],
        axis=1,
    )
    probe = jnp.concatenate(
        [
            shift_up(probe[:, :, cols - radius :], "fou"),
            probe,
            shift_down(probe[:, :, :radius], "fou"),
            jnp.zeros((channels, tall, LANES - 2 * radius), BF16),
        ],
        axis=2,
    )
    dual_next = analyse(probe, dual, ana_col, ana_row, thresholds)
    return (image_next, dual_next)


def solution(mesh):
    in_specs = (
        P(None, "img", "fou"),
        P(None, None, "img", "fou"),
        P(None, "img", "fou"),
        P(),
        P(),
        P("img"),
        P(None, "img", None),
        P(None, "img"),
        P(None, "img", None, None, None),
    )
    out_specs = (P(None, "img", "fou"), P(None, None, "img", "fou"))
    return jax.shard_map(body, mesh=mesh, in_specs=in_specs, out_specs=out_specs, check_vma=False)
```
